256 devices in a mesh: group: 8 (over x, core), expert: 32 (over y, z).
Axes of the slice: x: 4, y: 4, z: 8, core: 2. Of those that a mesh axis runs over, the one named last changes fastest.
Arguments:
- resid: bfloat16 [32768, 2048], P(('group', 'expert')), may hold values from -6 to 6
- queries: bfloat16 [32768, 2048], P(('group', 'expert')), may hold values from -48 to 48
- span_kv: bfloat16 [2, 32768, 2048], P(None, ('group', 'expert')), may hold values from -4 to 4
- cache_kv: bfloat16 [2, 256, 2, 128, 2048], P(None, ('group', 'expert')), may hold values from -6 to 6
- seg_len: int32 [256, 2], P(('group', 'expert')), may hold values from 0 to 128, as said below
- o_rows: bfloat16 [2048, 2048], P('expert'), may hold values from -0.125 to 0.125
- norm_gain: float32 [2048], replicated, may hold values from 0.25 to 1.75
- routes: int32 [32768, 8], P(('group', 'expert')), may hold values from 0 to 31, all different within a row; in each aligned block of 128 rows (0 to 127, 128 to 255, ...) at most 48 rows name the same one
- route_wts: float32 [32768, 8], P(('group', 'expert')), may hold values from 0.05 to 0.6
- w_in: bfloat16 [32, 2048, 1024], P('expert'), may hold values from -0.125 to 0.125
- w_out: bfloat16 [32, 512, 2048], P('expert'), may hold values from -0.25 to 0.25
Outputs:
- layer_out: bfloat16 [32768, 2048], P(('group', 'expert'))
The draws below stay inside these ranges and needn't reach their ends.
Inputs may be any that keep to these rules, and one draw needn't show every extreme that they name: seg_len[d, 0] is 1 to 128; seg_len[d, 1] is 0 (the paired request is short) or 1 to 128; seg_len[0, 0] and seg_len[0, 1] are 128 and seg_len[1, 1] is 0. `routes`: each row names 8 different experts; among the 128 rows of one device no expert is named more than 48 times.
All inputs are finite; a program needn't handle non-finite values.
Results may differ from the reference program's by a relative error of at most 0.0053.
Values may be sent and summed in bfloat16 or wider, within the bound.
A program may use at most 128 MiB of HBM per device.

```python
import math
import jax
import jax.numpy as jnp
import numpy as np
from jax import lax

HEADS = 16
HD = 128
D = 2048
FF = 512
TOPK = 8
SPAN = 128
SEG = 128
EXPERTS = 32
CAP = 48
DEVS = 256
TOKENS = 32768
N_GROUP = 8
N_EXPERT = 32


def joint_rows(key):
    key_q, key_k, key_v = jax.random.split(jax.random.fold_in(key, 7), 3)
    keys_raw = jnp.clip(jax.random.normal(key_k, (TOKENS, D), jnp.float32), -4.0, 4.0)
    queries_raw = jnp.clip(jax.random.normal(key_q, (TOKENS, D), jnp.float32), -4.0, 4.0)
    values_raw = jnp.clip(jax.random.normal(key_v, (TOKENS, D), jnp.float32), -4.0, 4.0)
    return (queries_raw, keys_raw, values_raw)


def draw_queries(key, part):
    queries_raw, keys_raw, values_raw = joint_rows(key)
    return queries_raw.astype(jnp.bfloat16)


def draw_span_kv(key, part):
    queries_raw, keys_raw, values_raw = joint_rows(key)
    return jnp.stack([keys_raw, values_raw]).astype(jnp.bfloat16)


def draw_seg_len(key, part):
    key_own, key_long, key_part = jax.random.split(jax.random.fold_in(key, 11), 3)
    own_length = jax.random.randint(key_own, (DEVS,), 1, SEG + 1).astype(jnp.int32)
    own_length = own_length.at[0].set(SEG)
    is_long = jax.random.randint(key_long, (DEVS,), 0, 2).astype(jnp.int32)
    long_length = jax.random.randint(key_part, (DEVS,), 1, SEG + 1).astype(jnp.int32)
    second = jnp.where(is_long == 1, long_length, 0)
    second = second.at[0].set(SEG).at[1].set(0)
    return jnp.stack([own_length, second], axis=1).astype(jnp.int32)


def block_levels(own_key, shape, pieces, low, high):
    factor_of, own = 1.0, jax.random.fold_in(own_key, 6)
    for axis_at, parts in pieces:
        draws = jnp.exp(jax.random.uniform(jax.random.fold_in(own, axis_at), (parts,), jnp.float32, low / len(pieces), high / len(pieces)))
        factor_of = factor_of * jnp.repeat(draws, shape[axis_at] // parts).reshape([-1 if axis == axis_at else 1 for axis in range(len(shape))])
    return factor_of


def assign_block(own_key, own, number, rows, number_of, top, most, skew):
    sequence = jax.random.permutation(own_key, number_of)
    crowded, usual = load_shares(number_of, rows * top, most, skew, True), load_shares(number_of, rows * top, most, skew, False)
    places = jnp.arange(number_of)

    def named(lengths, offset_by):
        used = int((lengths > 0).sum())
        fixed = max(1, used // 4)
        passed = fixed + (places - fixed + offset_by * (used - fixed)) % max(1, number_of - fixed)
        return jnp.zeros((number_of,), jnp.int32).at[sequence[jnp.where(places < fixed, places, passed)]].set(jnp.asarray(lengths, jnp.int32))

    lengths = jnp.where(number % 4 == 0, named(crowded, number // 4), named(usual, number - number // 4 - 1))
    mixed = jax.random.permutation(jax.random.fold_in(own, 3), number_of)
    donor, receiver = mixed[0:number_of // 2 * 2:2], mixed[1:number_of // 2 * 2:2]
    room = jnp.minimum(lengths[donor] - 1, most - lengths[receiver]) // 2
    room = jnp.where((donor == sequence[0]) | (receiver == sequence[0]) | (lengths[receiver] == 0), 0, jnp.maximum(room, 0))
    passed = jax.random.randint(jax.random.fold_in(own, 4), (number_of // 2,), 0, 1 << 20) % (room + 1)
    lengths = lengths.at[donor].add(-passed).at[receiver].add(passed)
    members = jnp.searchsorted(jnp.cumsum(lengths), jnp.arange(rows * top), side="right").astype(jnp.int32)
    grid = members.reshape(top, rows).T
    grid = grid[jax.random.permutation(jax.random.fold_in(own, 1), rows)]
    offset_by = jax.random.randint(jax.random.fold_in(own, 2), (rows, 1), 0, top)
    return jnp.take_along_axis(grid, (jnp.arange(top)[None, :] + offset_by) % top, axis=1)


def load_shares(amount, total, bound, skew, full):
    loads = [(1 << 20) // math.isqrt(grade ** skew) + 1 for grade in range(1, amount + 1)]
    largest = bound if full else min(bound, max(-(-total // amount), total * loads[0] // sum(loads)))
    least = 1 if total - largest >= amount - 1 else 0
    holding, rest = [largest] + [least] * (amount - 1), total - largest - least * (amount - 1)
    while rest > 0:
        movable = [i for i in range(1, amount) if holding[i] < largest] or [i for i in range(1, amount) if holding[i] < bound]
        pool, budget = sum([loads[i] for i in movable]), rest
        for i in movable:
            addition = min(bound - holding[i], max(1, budget * loads[i] // pool), rest)
            holding[i] = holding[i] + addition
            rest = rest - addition
    return np.array(holding)


def scatter_about(own_key, extent, scale, limit, pieces=(), held_as=jnp.bfloat16):
    result = scale * jax.random.normal(own_key, extent, jnp.float32)
    if pieces:
        result = result * block_levels(own_key, extent, pieces, -0.22, 0.18)
    return jnp.clip(result, -limit, limit).astype(held_as)


def setup_inputs(seed: int = 0) -> dict:
    streams_of = jax.random.split(jax.random.key(seed), 12)
    resid = scatter_about(streams_of[0], (TOKENS, D), 1.0, 6.0, ((0, 256),))
    queries = draw_queries(jax.random.fold_in(streams_of[11], 71), 0)
    span_kv = draw_span_kv(jax.random.fold_in(streams_of[11], 71), 0)
    cache_kv = scatter_about(streams_of[3], (2, DEVS, 2, SEG, D), 1.0, 6.0, ((1, 256),))
    seg_len = draw_seg_len(jax.random.fold_in(streams_of[11], 71), 0)
    o_rows = scatter_about(streams_of[5], (D, D), D ** -0.5, 0.125, ((0, 32),))
    norm_gain = jnp.clip(1.0 + 0.15 * jax.random.normal(streams_of[6], (D,), jnp.float32), 0.25, 1.75)
    routes_keys = jax.random.split(jax.random.fold_in(streams_of[7], 1), TOKENS // SPAN)
    routes_turns = jax.random.permutation(jax.random.fold_in(streams_of[7], 3), TOKENS // SPAN)
    routes = jax.vmap(lambda own, number: assign_block(jax.random.fold_in(streams_of[7], 2), own, number, SPAN, EXPERTS, TOPK, CAP, 1))(routes_keys, routes_turns).reshape((TOKENS, TOPK))
    route_wts = jnp.clip(0.05 + 0.55 * jax.random.uniform(streams_of[8], (TOKENS, TOPK), jnp.float32) ** block_levels(streams_of[8], (TOKENS, TOPK), ((0, 256),), -0.2, 0.2), 0.05, 0.6)
    w_in = scatter_about(streams_of[9], (EXPERTS, D, 2 * FF), D ** -0.5, 0.125, ((0, 32),))
    w_out = scatter_about(streams_of[10], (EXPERTS, FF, D), FF ** -0.5, 0.25, ((0, 32),))
    return dict(resid=resid, queries=queries, span_kv=span_kv, cache_kv=cache_kv, seg_len=seg_len, o_rows=o_rows, norm_gain=norm_gain, routes=routes, route_wts=route_wts, w_in=w_in, w_out=w_out)


def attend(query_rows, key_rows, value_rows, valid_keys):
    q_heads = query_rows.astype(jnp.float32).reshape(-1, HEADS, HD)
    k_heads = key_rows.astype(jnp.float32).reshape(-1, HEADS, HD)
    v_heads = value_rows.astype(jnp.float32).reshape(-1, HEADS, HD)
    scores = jnp.einsum('chd,shd->hcs', q_heads, k_heads) * (1.0 / math.sqrt(HD))
    scores = jnp.where(valid_keys[None, None, :], scores, -1e+30)
    peak_score = lax.optimization_barrier(jnp.max(scores, axis=-1))
    expo = jnp.where(valid_keys[None, None, :], jnp.exp(scores - peak_score[..., None]), 0.0)
    totals = lax.optimization_barrier(jnp.sum(expo, axis=-1))
    probs_low = expo.astype(jnp.bfloat16).astype(jnp.float32)
    accum_out = jnp.einsum('hcs,shd->chd', probs_low, v_heads)
    return (peak_score, totals, accum_out)

def merge_parts(first, second):
    peak_a, total_a, accum_a = first
    peak_b, total_b, accum_b = second
    peak_both = jnp.maximum(peak_a, peak_b)
    scale_a = jnp.exp(peak_a - peak_both).T
    scale_b = jnp.exp(peak_b - peak_both).T
    numer = accum_a * scale_a[:, :, None] + accum_b * scale_b[:, :, None]
    denom = total_a.T * scale_a + total_b.T * scale_b
    merged = numer / denom[:, :, None]
    return merged.reshape(merged.shape[0], -1).astype(jnp.bfloat16)

def slot_of(route_rows):
    onehot = (route_rows[:, :, None] == jnp.arange(EXPERTS, dtype=jnp.int32)[None, None, :]).astype(jnp.int32)
    counts = lax.optimization_barrier(jnp.sum(onehot, axis=1))
    before = jnp.cumsum(counts, axis=0) - counts
    return lax.optimization_barrier(jnp.sum(onehot * before[:, None, :], axis=-1))

def expert_mlp(token_rows, weight_in, weight_out):
    joined = jnp.dot(token_rows, weight_in, preferred_element_type=jnp.float32)
    hidden = (jax.nn.silu(joined[:, :FF]) * joined[:, FF:]).astype(jnp.bfloat16)
    return jnp.dot(hidden, weight_out, preferred_element_type=jnp.float32).astype(jnp.bfloat16)

def reference(resid, queries, span_kv, cache_kv, seg_len, o_rows, norm_gain, routes, route_wts, w_in, w_out):
    query_blocks = queries.reshape(DEVS, SPAN, D)
    span_keys = span_kv[0].reshape(DEVS, SPAN, D)
    span_vals = span_kv[1].reshape(DEVS, SPAN, D)
    positions = jnp.arange(SEG, dtype=jnp.int32)

    def one_request(device):
        partner = jnp.bitwise_xor(device // N_EXPERT, 1) * N_EXPERT + device % N_EXPERT
        keys_a = jnp.concatenate([span_keys[device], cache_kv[0, device, 0]], axis=0)
        vals_a = jnp.concatenate([span_vals[device], cache_kv[1, device, 0]], axis=0)
        valid_a = jnp.concatenate([jnp.ones((SPAN,), bool), positions < seg_len[device, 0]])
        part_a = attend(query_blocks[device], keys_a, vals_a, valid_a)
        valid_b = positions < seg_len[partner, 1]
        part_b = attend(query_blocks[device], cache_kv[0, partner, 1], cache_kv[1, partner, 1], valid_b)
        return merge_parts(part_a, part_b)
    attended = lax.map(one_request, jnp.arange(DEVS, dtype=jnp.int32)).reshape(TOKENS, D)
    residual = resid.astype(jnp.float32) + jnp.dot(attended, o_rows, preferred_element_type=jnp.float32)
    normed = (residual * lax.rsqrt(lax.optimization_barrier(jnp.mean(residual * residual, axis=-1, keepdims=True)) + 1e-05) * norm_gain).astype(jnp.bfloat16)

    def one_group(group_id):
        start_row = (group_id * (N_EXPERT * SPAN)).astype(jnp.int32)
        group_acts = lax.dynamic_slice_in_dim(normed, start_row, N_EXPERT * SPAN, 0)
        group_resid = lax.dynamic_slice_in_dim(residual, start_row, N_EXPERT * SPAN, 0).reshape(N_EXPERT, SPAN, D)
        group_routes = lax.dynamic_slice_in_dim(routes, start_row, N_EXPERT * SPAN, 0).reshape(N_EXPERT, SPAN, TOPK)
        group_weights = lax.dynamic_slice_in_dim(route_wts, start_row, N_EXPERT * SPAN, 0).reshape(N_EXPERT, SPAN, TOPK)
        slot_ids = jax.vmap(slot_of)(group_routes)
        source = jnp.arange(N_EXPERT, dtype=jnp.int32)[:, None, None]
        buffer_pos = (group_routes * N_EXPERT + source) * CAP + slot_ids
        token_ids = jnp.broadcast_to(source * SPAN + jnp.arange(SPAN, dtype=jnp.int32)[None, :, None], buffer_pos.shape)
        slot_token = jnp.full((EXPERTS * N_EXPERT * CAP,), -1, jnp.int32).at[buffer_pos.reshape(-1)].set(token_ids.reshape(-1))
        token_rows = jnp.where((slot_token >= 0)[:, None], group_acts[jnp.maximum(slot_token, 0)], jnp.zeros((), jnp.bfloat16))
        token_rows = token_rows.reshape(EXPERTS, N_EXPERT * CAP, D)
        outputs = lax.map(lambda items: expert_mlp(items[0], items[1], items[2]), (token_rows, w_in, w_out))
        outputs = outputs.reshape(EXPERTS * N_EXPERT * CAP, D)
        expert_sum = jnp.zeros((N_EXPERT, SPAN, D), jnp.float32)
        for route_k in range(TOPK):
            picked = outputs[buffer_pos[:, :, route_k]].astype(jnp.float32)
            expert_sum = expert_sum + group_weights[:, :, route_k, None] * picked
        return (group_resid + expert_sum).astype(jnp.bfloat16).reshape(N_EXPERT * SPAN, D)
    layer_out = lax.map(one_group, jnp.arange(N_GROUP, dtype=jnp.int32))
    return layer_out.reshape(TOKENS, D)
```

```python
import math

import jax
import jax.numpy as jnp
from jax import lax
from jax.experimental import pallas as pl
from jax.experimental.pallas import tpu as pltpu
from jax.sharding import PartitionSpec as P

MESH = pl.DeviceIdType.MESH
HEADS = 16
HD = 128
D = 2048
FF = 512
TOPK = 8
SPAN = 128
NX, NY, NZ = 4, 4, 8
WIDE = D + 128
F32 = jnp.float32
BF16 = jnp.bfloat16
REL = (2, 1, 3, 0)


def seq(i):
    return (2 + 3 * i + 3 * (i // 2) + 2 * (i // 3)) % 4


def layer_kernel(
    q_hbm, span_hbm, cache_hbm, resid_hbm, o_hbm, win_hbm, wout_hbm,
    len_ref, routes_ref, wts_ref, gain_ref,
    out_ref,
    q, kk, vv, resid, plen, bias, att, obuf, proj, proj_in, res,
    wi, wo, xbuf, qbuf, hid, r1, r2, r3, r4,
    loc, pk_s, pk_r, sc_s, sc_r, oz_s, oz_r, o2_s, o2_r, o3_s, o3_r, at_s, at_r,
    pr_s, pr_r, w_s, w_r, g1_s, g1_r, g2_s, g2_r, g3_s, g3_r, g4_s, g4_r, gp_s, gp_r,
    q_s, q_r, r1_s, r1_r, r2_s, r2_r, r3_s, r3_r, r4_s, r4_r,
):
    g = lax.axis_index("group")
    e = lax.axis_index("expert")
    x, c = g // 2, g % 2
    y, z = e // NZ, e % NZ
    oc = 1 - c

    def dev(x_=x, c_=c, y_=y, z_=z):
        return (x_ * 2 + c_, y_ * NZ + z_)

    partner = dev(c_=oc)
    twin = (z, y * NZ + g)

    def rc(src, dst, ss, rs, to):
        return pltpu.make_async_remote_copy(
            src_ref=src, dst_ref=dst, send_sem=ss, recv_sem=rs, device_id=to, device_id_type=MESH
        )

    sent = []

    def send(src, dst, ss, rs, to, keep=None):
        copy = rc(src, dst, ss, rs, to)
        copy.start()
        (sent if keep is None else keep).append(copy)

    def landed(dst, ss, rs):
        rc(dst, dst, ss, rs, partner).wait_recv()

    loads = [
        pltpu.make_async_copy(q_hbm, q, loc.at[0]),
        pltpu.make_async_copy(span_hbm.at[0], kk.at[pl.ds(0, 128)], loc.at[1]),
        pltpu.make_async_copy(span_hbm.at[1], vv.at[pl.ds(0, 128)], loc.at[2]),
        pltpu.make_async_copy(cache_hbm.at[0, 0, 0], kk.at[pl.ds(128, 128)], loc.at[3]),
        pltpu.make_async_copy(cache_hbm.at[1, 0, 0], vv.at[pl.ds(128, 128)], loc.at[4]),
        pltpu.make_async_copy(resid_hbm, resid, loc.at[5]),
    ]
    for load in loads:
        load.start()
    half_cols = pl.ds(pl.multiple_of(c * 1024, 128), 1024)
    other_cols = pl.ds(pl.multiple_of(oc * 1024, 128), 1024)
    my16 = pl.ds(pl.multiple_of(x * 16, 16), 16)
    own_o = pltpu.make_async_copy(o_hbm.at[my16, half_cols], obuf.at[y, z, my16], loc.at[6])
    own_o.start()

    barrier = pltpu.get_barrier_semaphore()
    greet = [partner]
    greet += [dev(x_=(x + d) % NX) for d in range(1, NX)]
    greet += [dev(y_=(y + d) % NY) for d in range(1, NY)]
    greet += [dev(z_=(z + d) % NZ) for d in range(1, NZ)]
    for peer in greet:
        pl.semaphore_signal(barrier, inc=1, device_id=peer, device_id_type=MESH)

    @pl.when(z != g)
    def _():
        pl.semaphore_signal(barrier, inc=1, device_id=twin, device_id_type=MESH)
        pl.semaphore_wait(barrier, len(greet) + 1)

    @pl.when(z == g)
    def _():
        pl.semaphore_wait(barrier, len(greet))

    send(cache_hbm.at[0, 0, 1], kk.at[pl.ds(256, 128)], pk_s.at[0], pk_r.at[0], partner)
    send(cache_hbm.at[1, 0, 1], vv.at[pl.ds(256, 128)], pk_s.at[1], pk_r.at[1], partner)
    send(len_ref.at[1], plen, pk_s.at[2], pk_r.at[2], partner)

    for d in range(1, NZ):
        send(
            o_hbm.at[my16, half_cols], obuf.at[y, z, my16],
            oz_s.at[d - 1], oz_r.at[d - 1], dev(z_=(z + d) % NZ),
        )

    src_i = pl.ds(pl.multiple_of(g * 256, 256), 256)
    src_o = pl.ds(pl.multiple_of(g * 64, 64), 64)
    dst_i = pl.ds(pl.multiple_of(z * 256, 256), 256)
    dst_o = pl.ds(pl.multiple_of(z * 64, 64), 64)
    twin_copies = (
        rc(win_hbm.at[0, src_i], wi.at[src_i], sc_s.at[0], sc_r.at[0], twin),
        rc(wout_hbm.at[0, src_o], wo.at[src_o], sc_s.at[1], sc_r.at[1], twin),
    )
    self_copies = (
        pltpu.make_async_copy(win_hbm.at[0, dst_i], wi.at[dst_i], sc_r.at[0]),
        pltpu.make_async_copy(wout_hbm.at[0, dst_o], wo.at[dst_o], sc_r.at[1]),
    )

    @pl.when(z != g)
    def _():
        for copy in twin_copies:
            copy.start()

    @pl.when(z == g)
    def _():
        for copy in self_copies:
            copy.start()

    def twin_wait():
        @pl.when(z != g)
        def _():
            landed(wi.at[dst_i], sc_s.at[0], sc_r.at[0])
            landed(wo.at[dst_o], sc_s.at[1], sc_r.at[1])

        @pl.when(z == g)
        def _():
            for copy in self_copies:
                copy.wait()

    def part(way, owner):
        rows_i = pl.ds(pl.multiple_of(owner * 256 + way * 128, 128), 128)
        rows_o = pl.ds(pl.multiple_of(owner * 64 + way * 32, 32), 32)
        return wi.at[rows_i], wo.at[rows_o]

    def ring_send(step):
        for way, sign in ((0, 1), (1, -1)):
            owner = (z - sign * (step - 1) + NZ) % NZ
            to = dev(z_=(z + sign + NZ) % NZ)
            for k, ref in enumerate(part(way, owner)):
                send(ref, ref, w_s.at[way, step - 1, k], w_r.at[way, step - 1, k], to)

    def ring_wait(step):
        for way, sign in ((0, 1), (1, -1)):
            owner = (z - sign * step + NZ) % NZ
            for k, ref in enumerate(part(way, owner)):
                landed(ref, w_s.at[way, step - 1, k], w_r.at[way, step - 1, k])

    def ring(step):
        ring_wait(step)
        if step < NZ - 1:
            ring_send(step + 1)

    def o_stage2():
        own_o.wait()
        for d in range(1, NZ):
            ref = obuf.at[y, (z - d + NZ) % NZ, my16]
            landed(ref, oz_s.at[d - 1], oz_r.at[d - 1])
        for u in range(2):
            ref = obuf.at[y, :, my16, pl.ds(512 * u, 512)]
            for d in range(1, 4):
                to = dev(x_=(x + d) % NX) if u == 0 else dev(y_=(y + d) % NY)
                send(ref, ref, o2_s.at[u, d - 1], o2_r.at[u, d - 1], to)

    def o_stage3():
        for u in range(2):
            for d in range(1, 4):
                if u == 0:
                    from16 = pl.ds(pl.multiple_of((x - d + NX) % NX * 16, 16), 16)
                    ref = obuf.at[y, :, from16, pl.ds(0, 512)]
                else:
                    ref = obuf.at[(y - d + NY) % NY, :, my16, pl.ds(512, 512)]
                landed(ref, o2_s.at[u, d - 1], o2_r.at[u, d - 1])
        for u in range(2):
            for d in range(1, 4):
                if u == 0:
                    ref, to = obuf.at[y, :, :, pl.ds(0, 512)], dev(y_=(y + d) % NY)
                else:
                    ref, to = obuf.at[:, :, my16, pl.ds(512, 512)], dev(x_=(x + d) % NX)
                send(ref, ref, o3_s.at[u, d - 1], o3_r.at[u, d - 1], to)

    def o_finish():
        for u in range(2):
            for d in range(1, 4):
                if u == 0:
                    ref = obuf.at[(y - d + NY) % NY, :, :, pl.ds(0, 512)]
                else:
                    from16 = pl.ds(pl.multiple_of((x - d + NX) % NX * 16, 16), 16)
                    ref = obuf.at[:, :, from16, pl.ds(512, 512)]
                landed(ref, o3_s.at[u, d - 1], o3_r.at[u, d - 1])

    for load in loads:
        load.wait()
    o_stage2()
    landed(kk.at[pl.ds(256, 128)], pk_s.at[0], pk_r.at[0])
    landed(vv.at[pl.ds(256, 128)], pk_s.at[1], pk_r.at[1])
    landed(plen, pk_s.at[2], pk_r.at[2])
    lane = lax.broadcasted_iota(jnp.int32, (8, 128), 1)
    bias[:, 0:128] = jnp.zeros((8, 128), F32)
    bias[:, 128:256] = jnp.where(lane < len_ref[0], 0.0, -1e30)
    bias[:, 256:384] = jnp.where(lane < plen[...], 0.0, -1e30)

    def heads(i):
        for j in range(2):
            cols = pl.ds(pl.multiple_of(i * 256 + j * 128, 128), 128)
            s = lax.dot_general(
                q[:, cols], kk[:, cols], (((1,), (1,)), ((), ())), preferred_element_type=F32
            )
            s = s * (1.0 / math.sqrt(HD)) + bias[0:1, :]
            m = jnp.max(s, axis=-1, keepdims=True)
            p = jnp.exp(s - m)
            total = jnp.sum(p, axis=-1, keepdims=True)
            a = jnp.dot(p.astype(BF16), vv[:, cols], preferred_element_type=F32)
            att[c, :, cols] = (a / total).astype(BF16)

    def head_range(low, high):
        @pl.loop(low, high)
        def _(i):
            heads(i)

    head_range(0, 4)
    o_stage3()
    head_range(4, 8)
    send(att.at[c], att.at[c], at_s.at[0], at_r.at[0], partner)
    twin_wait()
    ring_send(1)

    lanes = lax.broadcasted_iota(jnp.int32, (SPAN, 128), 1)
    gate_all = jnp.zeros((SPAN, 128), F32)
    for k in range(TOPK):
        gate_all += jnp.where(lanes == routes_ref[:, k:k + 1], wts_ref[:, k:k + 1], 0.0)
    xbuf[c, x, y, :, D:] = gate_all.astype(BF16)

    landed(att.at[oc], at_s.at[0], at_r.at[0])
    o_finish()
    both = 2 * SPAN

    @pl.loop(0, 2)
    def _(t):
        cols = pl.ds(pl.multiple_of(t * 512, 512), 512)
        proj[:, :, cols] = jnp.dot(
            att[...].reshape(both, D), obuf[:, :, :, cols].reshape(D, 512),
            preferred_element_type=F32,
        ).reshape(2, SPAN, 512)

    send(proj.at[oc], proj_in, pr_s.at[0], pr_r.at[0], partner)
    res[:, half_cols] = resid[:, half_cols].astype(F32) + proj[c]
    landed(proj_in, pr_s.at[0], pr_r.at[0])
    res[:, other_cols] = resid[:, other_cols].astype(F32) + proj_in[...]

    @pl.loop(0, 4)
    def _(t):
        rows = pl.ds(pl.multiple_of(t * 32, 32), 32)
        r = res[rows, :]
        scale = lax.rsqrt(jnp.mean(r * r, axis=-1, keepdims=True) + 1e-05)
        xbuf[c, x, y, rows, 0:D] = (r * scale * gain_ref[...]).astype(BF16)

    gathers = []

    def axis_of(hf, first):
        return (x, y)[hf ^ (not first)]

    def xy(hf, o, p):
        return (o, p) if hf == 0 else (p, o)

    def step(hf, on_o, d):
        if (hf == 0) == on_o:
            return dev(x_=(x + d) % 4)
        return dev(y_=(y + d) % 4)

    def mine(hf):
        return (x, y) if hf == 0 else (y, x)

    def piece(hf, j, k, low=0, size=64):
        o, p = mine(hf)
        xx, yy = xy(hf, (o + j) % 4, (p + k) % 4)
        return xbuf.at[c, xx, yy, pl.ds(64 * hf + low, size)]

    def gather_send(hf, j, k, low, size, on_o, d, ss, rs):
        ref = piece(hf, j, k, low, size)
        send(ref, ref, ss, rs, step(hf, on_o, d), gathers)

    def to_partner(hf, j, k):
        ref = piece(hf, j, k)
        send(ref, ref, gp_s.at[hf, j, k], gp_r.at[hf, j, k], partner, gathers)

    def first_over(hf):
        for w, d in ((0, 1), (1, 3)):
            gather_send(hf, 0, 0, 0, 64, True, d, g1_s.at[hf, w], g1_r.at[hf, w])

    def then_over(hf, j):
        for w, d in ((0, 1), (1, 3)):
            gather_send(hf, j, 0, 0, 64, False, d, g3_s.at[hf, j, w], g3_r.at[hf, j, w])
        to_partner(hf, j, 0)

    def first_pass(hf):
        for w, d in ((0, 1), (1, 3)):
            landed(piece(hf, 4 - d, 0), g1_s.at[hf, w], g1_r.at[hf, w])
            gather_send(hf, 4 - d, 0, 32 * w, 32, True, d, g2_s.at[hf, w], g2_r.at[hf, w])
        for d in (1, 3):
            then_over(hf, 4 - d)

    def first_end(hf):
        for w in range(2):
            landed(piece(hf, 2, 0, 32 * w, 32), g2_s.at[hf, w], g2_r.at[hf, w])
        then_over(hf, 2)

    def then_pass(hf, j):
        for w, d in ((0, 1), (1, 3)):
            landed(piece(hf, j, 4 - d), g3_s.at[hf, j, w], g3_r.at[hf, j, w])
            gather_send(hf, j, 4 - d, 32 * w, 32, False, d, g4_s.at[hf, j, w], g4_r.at[hf, j, w])
        for d in (1, 3):
            to_partner(hf, j, 4 - d)

    def then_end(hf, j):
        for w in range(2):
            landed(piece(hf, j, 2, 32 * w, 32), g4_s.at[hf, j, w], g4_r.at[hf, j, w])
        to_partner(hf, j, 2)

    for hf in range(2):
        first_over(hf)
    for hf in range(2):
        then_over(hf, 0)
    ring(1)
    for hf in range(2):
        first_pass(hf)
    for hf in range(2):
        then_pass(hf, 0)
    ring(2)
    for hf in range(2):
        first_end(hf)
    for j in (1, 3):
        for hf in range(2):
            then_pass(hf, j)
        ring(3 if j == 1 else 4)
    for hf in range(2):
        then_pass(hf, 2)
    ring(5)
    for j in (0, 1, 3, 2):
        for hf in range(2):
            then_end(hf, j)
        if j == 1:
            ring(6)
    for hf in range(2):
        o, p = mine(hf)
        for j in range(4):
            for k in range(4):
                xx, yy = xy(hf, (o + j) % 4, (p + k) % 4)
                landed(xbuf.at[oc, xx, yy, pl.ds(64 * hf, 64)], gp_s.at[hf, j, k], gp_r.at[hf, j, k])
    for copy in gathers:
        copy.wait_send()
    ring(7)

    me = y * NZ + g

    def result_copy(xx, yy):
        return rc(
            xbuf.at[oc, xx, yy, :, pl.ds(0, D)], qbuf.at[xx, yy],
            q_s.at[xx * 4 + yy], q_r.at[xx * 4 + yy], partner,
        )

    def expert_block(xx, yy):
        @pl.loop(0, 2)
        def _(t):
            left = pl.ds(pl.multiple_of(t * 256, 256), 256)
            right = pl.ds(pl.multiple_of(t * 256 + 512, 256), 256)
            rows = xbuf[:, xx, yy, :, 0:D].reshape(both, D)
            gate = jnp.dot(rows, wi[:, left], preferred_element_type=F32)
            up = jnp.dot(rows, wi[:, right], preferred_element_type=F32)
            hid[:, left] = (jax.nn.silu(gate) * up).astype(BF16)

        gates = xbuf[:, xx, yy, :, D:].reshape(both, 128).astype(F32)
        pick = lax.broadcasted_iota(jnp.int32, (both, 128), 1) == me
        weight = jnp.sum(jnp.where(pick, gates, 0.0), axis=-1, keepdims=True)

        @pl.loop(0, 4)
        def _(t):
            cols = pl.ds(pl.multiple_of(t * 512, 512), 512)
            part_out = jnp.dot(hid[...], wo[:, cols], preferred_element_type=F32) * weight
            xbuf[:, xx, yy, :, cols] = part_out.astype(BF16).reshape(2, SPAN, 512)

        result_copy(xx, yy).start()

    def add_partner(xx, yy):
        landed(qbuf.at[xx, yy], q_s.at[xx * 4 + yy], q_r.at[xx * 4 + yy])

        @pl.loop(0, 4)
        def _(t):
            rows = pl.ds(pl.multiple_of(t * 32, 32), 32)
            total = xbuf[c, xx, yy, rows, 0:D].astype(F32) + qbuf[xx, yy, rows].astype(F32)
            xbuf[c, xx, yy, rows, 0:D] = total.astype(BF16)

    def run(blocks, body):
        count, place = blocks

        @pl.loop(0, count)
        def _(i):
            dx, dy = place(i)
            body((x + dx) % 4, (y + dy) % 4)

    batches = (
        (4, lambda i: (seq(i), 2)),
        (3, lambda i: (2, seq(i + 1))),
        (3, lambda i: (1, seq(i + 1))),
        (3, lambda i: (3, seq(i + 1))),
        (3, lambda i: (0, seq(i + 1))),
    )

    def sums(hf, j, k, low=0, size=64):
        o, p = mine(hf)
        xx, yy = xy(hf, (o + j) % 4, (p + k) % 4)
        return xbuf.at[c, xx, yy, pl.ds(64 * hf + low, size), pl.ds(0, D)]

    def add_into(target, *terms):
        total = target[...].astype(F32)
        for term in terms:
            total += term[...].astype(F32)
        target[...] = total.astype(BF16)

    def back1(hf, j):
        for w, d in ((0, 1), (1, 3)):
            send(
                sums(hf, j, 2, 32 * w, 32), r1.at[hf, w, j],
                r1_s.at[hf, w, j], r1_r.at[hf, w, j], step(hf, False, d),
            )

    def back2(hf, j):
        for w, d in ((0, 1), (1, 3)):
            landed(r1.at[hf, w, j], r1_s.at[hf, w, j], r1_r.at[hf, w, j])
            add_into(sums(hf, j, d, 32 * w, 32), r1.at[hf, w, j])
        for w, d in ((0, 1), (1, 3)):
            send(
                sums(hf, j, d), r2.at[hf, w, j],
                r2_s.at[hf, w, j], r2_r.at[hf, w, j], step(hf, False, d),
            )

    def back3(hf, j):
        for w in range(2):
            landed(r2.at[hf, w, j], r2_s.at[hf, w, j], r2_r.at[hf, w, j])
        add_into(sums(hf, j, 0), r2.at[hf, 0, j], r2.at[hf, 1, j])

    def home1(hf):
        for w, d in ((0, 1), (1, 3)):
            send(
                sums(hf, 2, 0, 32 * w, 32), r3.at[hf, w],
                r3_s.at[hf, w], r3_r.at[hf, w], step(hf, True, d),
            )

    def home2(hf):
        for w, d in ((0, 1), (1, 3)):
            landed(r3.at[hf, w], r3_s.at[hf, w], r3_r.at[hf, w])
            add_into(sums(hf, d, 0, 32 * w, 32), r3.at[hf, w])
        for w, d in ((0, 1), (1, 3)):
            send(
                sums(hf, d, 0), r4.at[hf, w],
                r4_s.at[hf, w], r4_r.at[hf, w], step(hf, True, d),
            )

    def home3(hf):
        for w in range(2):
            landed(r4.at[hf, w], r4_s.at[hf, w], r4_r.at[hf, w])
        rows = pl.ds(64 * hf, 64)
        total = sums(hf, 0, 0)[...].astype(F32) + r4[hf, 0].astype(F32) + r4[hf, 1].astype(F32)
        out_ref[rows, :] = (res[rows, :] + total).astype(BF16)

    run(batches[0], expert_block)
    run(batches[1], expert_block)
    run(batches[0], add_partner)
    for j in REL:
        back1(0, j)
    run(batches[2], expert_block)
    run(batches[1], add_partner)
    for j in REL:
        back1(1, j)
    back2(0, 2)
    run(batches[3], expert_block)
    run(batches[2], add_partner)
    back2(0, 1)
    run(batches[4], expert_block)
    run(batches[3], add_partner)
    back2(1, 2)
    back2(0, 3)
    back2(1, 1)
    back2(1, 3)
    back2(1, 0)
    run(batches[4], add_partner)
    back2(0, 0)
    for hf in range(2):
        back3(hf, 2)
        home1(hf)
    for hf in range(2):
        back3(hf, 1)
        back3(hf, 3)
        home2(hf)
    for hf in range(2):
        back3(hf, 0)
    for hf in range(2):
        home3(hf)

    @pl.when(z != g)
    def _():
        for copy in twin_copies:
            copy.wait_send()

    @pl.loop(0, 16)
    def _(i):
        result_copy(i // 4, i % 4).wait_send()

    for copy in sent:
        copy.wait_send()


def shards(
    resid, queries, span_kv, cache_kv, seg_len, o_rows, norm_gain, routes, route_wts, w_in, w_out
):
    lens = jnp.broadcast_to(seg_len[0][:, None, None], (2, 8, 128))
    dma = pltpu.SemaphoreType.DMA
    vmem = pltpu.VMEM
    hbm = pl.BlockSpec(memory_space=pl.ANY)
    local = pl.BlockSpec(memory_space=pltpu.VMEM)
    return pl.pallas_call(
        layer_kernel,
        out_shape=jax.ShapeDtypeStruct((SPAN, D), BF16),
        in_specs=[hbm] * 7 + [local] * 4,
        out_specs=local,
        scratch_shapes=[
            vmem((SPAN, D), BF16),
            vmem((3 * SPAN, D), BF16),
            vmem((3 * SPAN, D), BF16),
            vmem((SPAN, D), BF16),
            vmem((8, 128), jnp.int32),
            vmem((8, 384), F32),
            vmem((2, SPAN, D), BF16),
            vmem((NY, NZ, 64, 1024), BF16),
            vmem((2, SPAN, 1024), F32),
            vmem((SPAN, 1024), F32),
            vmem((SPAN, D), F32),
            vmem((D, 2 * FF), BF16),
            vmem((FF, D), BF16),
            vmem((2, NX, NY, SPAN, WIDE), BF16),
            vmem((NX, NY, SPAN, D), BF16),
            vmem((2 * SPAN, FF), BF16),
            vmem((2, 2, 4, 32, D), BF16),
            vmem((2, 2, 4, 64, D), BF16),
            vmem((2, 2, 32, D), BF16),
            vmem((2, 2, 64, D), BF16),
            dma((7,)), dma((3,)), dma((3,)), dma((2,)), dma((2,)),
            dma((7,)), dma((7,)), dma((2, 3)), dma((2, 3)), dma((2, 3)), dma((2, 3)),
            dma((1,)), dma((1,)), dma((1,)), dma((1,)),
            dma((2, 7, 2)), dma((2, 7, 2)),
            dma((2, 2)), dma((2, 2)), dma((2, 2)), dma((2, 2)),
            dma((2, 4, 2)), dma((2, 4, 2)), dma((2, 4, 2)), dma((2, 4, 2)),
            dma((2, 4, 4)), dma((2, 4, 4)),
            dma((16,)), dma((16,)),
            dma((2, 2, 4)), dma((2, 2, 4)), dma((2, 2, 4)), dma((2, 2, 4)),
            dma((2, 2)), dma((2, 2)), dma((2, 2)), dma((2, 2)),
        ],
        compiler_params=pltpu.CompilerParams(
            collective_id=0, has_side_effects=True, vmem_limit_bytes=67043328
        ),
    )(
        queries, span_kv, cache_kv, resid, o_rows, w_in, w_out,
        lens, routes, route_wts, norm_gain.reshape(1, D),
    )


def solution(mesh):
    placed = (
        P(("group", "expert"), None),
        P(("group", "expert"), None),
        P(None, ("group", "expert"), None),
        P(None, ("group", "expert"), None, None, None),
        P(("group", "expert"), None),
        P("expert", None),
        P(),
        P(("group", "expert"), None),
        P(("group", "expert"), None),
        P("expert", None, None),
        P("expert", None, None),
    )
    return jax.shard_map(
        shards, mesh=mesh, in_specs=placed, out_specs=P(("group", "expert"), None), check_vma=False
    )
```
